32 devices in a mesh: grp: 4 (over y, core), dp: 8 (over z, x).
Axes of the slice: x: 2, y: 2, z: 4, core: 2. Of those that a mesh axis runs over, the one named last changes fastest.
Arguments:
- hist_ids: int32 [256, 1024], P(('grp', 'dp')), may hold values from 0 to 262143, as said below
- hist_lens: int32 [256], P(('grp', 'dp')), may hold values from 1 to 1024
- cand_ids: int32 [256], P(('grp', 'dp')), may hold values from 0 to 262143, as said below
- labels: int32 [256], P(('grp', 'dp')), may hold values from 0 to 1
- item_table: float32 [262144, 256], P(('grp', 'dp')), may hold values from -6 to 6
- w_unit: float32 [512, 80], replicated, may hold values from -0.25 to 0.25
- b_unit: float32 [80], replicated, may hold values from -3 to 3
- w_mid: float32 [80, 40], replicated, may hold values from -0.625 to 0.625
- b_mid: float32 [40], replicated, may hold values from -3 to 3
- w_head: float32 [40, 4], replicated, may hold values from -1 to 1
- w_tower1: float32 [512, 200], replicated, may hold values from -0.25 to 0.25
- b_tower1: float32 [200], replicated, may hold values from -3 to 3
- w_tower2: float32 [200, 80], replicated, may hold values from -0.4375 to 0.4375
- b_tower2: float32 [80], replicated, may hold values from -3 to 3
- w_out: float32 [80], replicated, may hold values from -0.625 to 0.625
Outputs:
- grad_table: float32 [262144, 256], P(('grp', 'dp'))
- grad_w_unit: float32 [512, 80], replicated
- grad_b_unit: float32 [80], replicated
- grad_w_mid: float32 [80, 40], replicated
- grad_b_mid: float32 [40], replicated
- grad_w_head: float32 [40, 4], replicated
- grad_w_tower1: float32 [512, 200], replicated
- grad_b_tower1: float32 [200], replicated
- grad_w_tower2: float32 [200, 80], replicated
- grad_b_tower2: float32 [80], replicated
- grad_w_out: float32 [80], replicated
- loss: float32 [], replicated
The draws below stay inside these ranges and needn't reach their ends.
Inputs may be any that keep to these rules, and one draw needn't show every extreme that they name: Rows of item_table are owned in blocks of 8192 along grp+dp. Within one device's 8 users, the ids of hist_ids and cand_ids together fall at most 520 times into any one owner's block, and exactly 520 times into one owner's block in every draw. `cand_ids`: counted together with hist_ids, as promised there.
All inputs are finite; a program needn't handle non-finite values.
Results may differ from the reference program's by a relative error of at most 0.028.
Values may be sent and summed in bfloat16 or wider, within the bound.
A program may use at most 128 MiB of HBM per device.

```python
import math
import jax
import jax.numpy as jnp
from jax import lax

E = 256
HEADS = 4
U1 = 80
U2 = 40
T1 = 200
T2 = 80
HIST = 1024
TAB_DEV = 8192
BLOCK_USERS = 8
B_DEV = 8
VOCAB = 262144
BATCH = 256
CAP = 520
N_GRP = 4
N_DP = 8


def joint_ids(key):
    device_count = N_GRP * N_DP
    per_device = B_DEV * (HIST + 1)
    slot_total = device_count * CAP

    def one_device(dev_key):
        keys = jax.random.split(dev_key, 5)
        full_owner = jax.random.randint(keys[0], (), 0, device_count)
        ranking = jax.random.permutation(keys[1], slot_total).astype(jnp.int32)
        slot_numbers = jnp.arange(slot_total, dtype=jnp.int32)
        ordering = jnp.where(slot_numbers // CAP == full_owner, -1, ranking)
        chosen = jnp.argsort(ordering, stable=True)[:per_device].astype(jnp.int32)
        chosen = jax.random.permutation(keys[2], chosen)
        owner_of = chosen // CAP
        first_pick = jax.random.randint(keys[3], (per_device,), 0, TAB_DEV)
        second_pick = jax.random.randint(keys[4], (per_device,), 0, TAB_DEV)
        local_row = jnp.minimum(first_pick, second_pick)
        return (owner_of * TAB_DEV + local_row).astype(jnp.int32)
    dev_keys = jax.random.split(jax.random.fold_in(key, 4711), device_count)
    every_id = jax.vmap(one_device)(dev_keys)
    return every_id.reshape(BATCH, HIST + 1)


def draw_hist_ids(key, part):
    return joint_ids(key)[:, :HIST]


def draw_cand_ids(key, part):
    return joint_ids(key)[:, HIST]


def plant(values, stream_key, least, top_value):
    longest = values.shape.index(max(values.shape))
    spots = []
    for shift in (0, 1):
        where = [jax.random.randint(jax.random.fold_in(stream_key, axis), (), 0, length) for axis, length in enumerate(values.shape)]
        where[longest] = (where[longest] + shift) % values.shape[longest]
        spots.append(tuple(where))
    return values.at[spots[0]].set(least).at[spots[1]].set(top_value)


def levels(rng, shape, shards, smallest, top_value):
    def one(position, shards_of):
        heights = jax.random.uniform(jax.random.fold_in(jax.random.fold_in(rng, 6), position), (shards_of,), jnp.float32, smallest / len(shards), top_value / len(shards))
        return jnp.repeat(jnp.exp(heights), shape[position] // shards_of).reshape((-1,) + (1,) * (len(shape) - position - 1))

    loudness = one(*shards[0])
    for cut in shards[1:]:
        loudness = loudness * one(*cut)
    return loudness


def gaussian(own_key, extent, scale, bound, cuts=(), kind=jnp.bfloat16):
    array = jax.random.normal(own_key, extent, jnp.float32) * scale
    if len(cuts) > 0:
        array = levels(own_key, extent, cuts, -0.22, 0.18) * array
    return jnp.clip(array, min=-bound, max=bound).astype(kind)


def setup_inputs(seed: int = 0) -> dict:
    arg_keys = jax.random.split(jax.random.key(seed), 16)
    return {
        "hist_ids": draw_hist_ids(jax.random.fold_in(arg_keys[15], 71), 0),
        "hist_lens": plant(jax.random.randint(arg_keys[1], (BATCH,), 1, HIST + 1), jax.random.fold_in(arg_keys[1], 1), 1, HIST).astype(jnp.int32),
        "cand_ids": draw_cand_ids(jax.random.fold_in(arg_keys[15], 71), 0),
        "labels": plant(jax.random.randint(arg_keys[3], (BATCH,), 0, 2), jax.random.fold_in(arg_keys[3], 1), 0, 1).astype(jnp.int32),
        "item_table": gaussian(arg_keys[4], (VOCAB, E), 1.0, 6.0, ((0, 32),), jnp.float32),
        "w_unit": gaussian(arg_keys[5], (2 * E, U1), (2 * E) ** -0.5, 0.25, (), jnp.float32),
        "b_unit": gaussian(arg_keys[6], (U1,), 0.5, 3.0, (), jnp.float32),
        "w_mid": gaussian(arg_keys[7], (U1, U2), U1 ** -0.5, 0.625, (), jnp.float32),
        "b_mid": gaussian(arg_keys[8], (U2,), 0.5, 3.0, (), jnp.float32),
        "w_head": gaussian(arg_keys[9], (U2, HEADS), U2 ** -0.5, 1.0, (), jnp.float32),
        "w_tower1": gaussian(arg_keys[10], (2 * E, T1), (2 * E) ** -0.5, 0.25, (), jnp.float32),
        "b_tower1": gaussian(arg_keys[11], (T1,), 0.5, 3.0, (), jnp.float32),
        "w_tower2": gaussian(arg_keys[12], (T1, T2), T1 ** -0.5, 0.4375, (), jnp.float32),
        "b_tower2": gaussian(arg_keys[13], (T2,), 0.5, 3.0, (), jnp.float32),
        "w_out": gaussian(arg_keys[14], (T2,), T2 ** -0.5, 0.625, (), jnp.float32),
    }


def pool_block(unit_params, behavior_emb, block_lens, target):
    w_unit, b_unit, w_mid, b_mid, w_head = unit_params
    group_rows, hist_len, feat_width = behavior_emb.shape
    head_count = w_head.shape[1]
    crossed = (behavior_emb.astype(jnp.float32) * target[:, None, :].astype(jnp.float32)).astype(jnp.bfloat16)
    joined = jnp.concatenate([crossed, behavior_emb], axis=-1)
    first_pre = jnp.einsum('gle,ef->glf', joined.astype(jnp.float32), w_unit.astype(jnp.bfloat16).astype(jnp.float32)) + b_unit
    act_one = jax.nn.silu(first_pre).astype(jnp.bfloat16)
    second = jnp.einsum('glf,fk->glk', act_one.astype(jnp.float32), w_mid.astype(jnp.bfloat16).astype(jnp.float32)) + b_mid
    act_two = jax.nn.silu(second).astype(jnp.bfloat16)
    scores = jnp.einsum('glk,kh->glh', act_two.astype(jnp.float32), w_head.astype(jnp.bfloat16).astype(jnp.float32))
    live_mask = lax.broadcasted_iota(jnp.int32, (group_rows, hist_len), 1) < block_lens[:, None]
    weight = (jnp.where(live_mask[:, :, None], scores, 0.0) * (1.0 / math.sqrt(hist_len))).astype(jnp.bfloat16)
    head_parts = behavior_emb.reshape(group_rows, hist_len, head_count, feat_width // head_count)
    pooled = jnp.einsum('glh,glhd->ghd', weight.astype(jnp.float32), head_parts.astype(jnp.float32))
    return pooled.reshape(group_rows, feat_width)

def tower_loss(tower_params, pooled, target, labels, loss_scale):
    w_tower1, b_tower1, w_tower2, b_tower2, w_out = tower_params
    feature = jnp.concatenate([pooled, target.astype(jnp.float32)], axis=-1).astype(jnp.bfloat16)
    hidden_one = jax.nn.silu(jnp.dot(feature, w_tower1.astype(jnp.bfloat16), preferred_element_type=jnp.float32) + b_tower1).astype(jnp.bfloat16)
    hidden_two = jax.nn.silu(jnp.dot(hidden_one, w_tower2.astype(jnp.bfloat16), preferred_element_type=jnp.float32) + b_tower2).astype(jnp.bfloat16)
    logits = jnp.dot(hidden_two, w_out.astype(jnp.bfloat16), preferred_element_type=jnp.float32)
    losses = jax.nn.softplus(logits) - labels.astype(jnp.float32) * logits
    return jnp.sum(losses) * loss_scale

def total_loss(behavior_emb, target, unit_params, tower_params, hist_lens, labels, loss_scale):
    user_count, hist_len, feat_width = behavior_emb.shape
    block_count = user_count // BLOCK_USERS
    block_args = (behavior_emb.reshape(block_count, BLOCK_USERS, hist_len, feat_width), hist_lens.reshape(block_count, BLOCK_USERS), target.reshape(block_count, BLOCK_USERS, feat_width))
    one_block = jax.checkpoint(lambda parts_in: pool_block(unit_params, parts_in[0], parts_in[1], parts_in[2]))
    pooled = lax.map(one_block, block_args).reshape(user_count, feat_width)
    return tower_loss(tower_params, pooled, target, labels, loss_scale)

def reference(hist_ids, hist_lens, cand_ids, labels, item_table, w_unit, b_unit, w_mid, b_mid, w_head, w_tower1, b_tower1, w_tower2, b_tower2, w_out):
    loss_scale = 1.0 / math.sqrt(BATCH)
    unit_params = (w_unit, b_unit, w_mid, b_mid, w_head)
    tower_params = (w_tower1, b_tower1, w_tower2, b_tower2, w_out)
    block_count = BATCH // BLOCK_USERS
    block_ids = hist_ids.reshape(block_count, BLOCK_USERS * HIST)
    behavior_emb = lax.map(lambda these_ids: item_table[these_ids].astype(jnp.bfloat16), block_ids).reshape(BATCH, HIST, E)
    target = item_table[cand_ids].astype(jnp.bfloat16)

    def loss_of(emb_in, target_in, unit_in, tower_in):
        return total_loss(emb_in, target_in, unit_in, tower_in, hist_lens, labels, loss_scale)
    loss, pullback = jax.vjp(loss_of, behavior_emb, target, unit_params, tower_params)
    d_emb, d_target, unit_grads, tower_grads = pullback(jnp.ones((), loss.dtype))

    def add_block(running, block_in):
        these_ids, these_cot = block_in
        return (running.at[these_ids].add(these_cot.astype(jnp.float32)), None)
    start_grad = jnp.zeros((VOCAB, E), jnp.float32)
    grad_table, unused = lax.scan(add_block, start_grad, (block_ids, d_emb.reshape(block_count, BLOCK_USERS * HIST, E)))
    grad_table = grad_table.at[cand_ids].add(d_target.astype(jnp.float32))
    grad_table = grad_table * float(HIST)
    return (grad_table, unit_grads[0], unit_grads[1], unit_grads[2], unit_grads[3], unit_grads[4], tower_grads[0], tower_grads[1], tower_grads[2], tower_grads[3], tower_grads[4], loss)
```

```python
import math

import jax
import jax.numpy as jnp
from jax import lax
from jax.sharding import PartitionSpec as P

BLOCK_USERS = 8


def pool_block(unit_params, behavior_emb, block_lens, target):
    w_unit, b_unit, w_mid, b_mid, w_head = unit_params
    group_rows, hist_len, feat_width = behavior_emb.shape
    head_count = w_head.shape[1]
    crossed = (behavior_emb.astype(jnp.float32) * target[:, None, :].astype(jnp.float32)).astype(
        jnp.bfloat16
    )
    joined = jnp.concatenate([crossed, behavior_emb], axis=-1)
    first_pre = (
        jnp.einsum(
            "gle,ef->glf", joined, w_unit.astype(jnp.bfloat16), preferred_element_type=jnp.float32
        )
        + b_unit
    )
    act_one = jax.nn.silu(first_pre).astype(jnp.bfloat16)
    second = (
        jnp.einsum(
            "glf,fk->glk", act_one, w_mid.astype(jnp.bfloat16), preferred_element_type=jnp.float32
        )
        + b_mid
    )
    act_two = jax.nn.silu(second).astype(jnp.bfloat16)
    scores = jnp.einsum(
        "glk,kh->glh", act_two, w_head.astype(jnp.bfloat16), preferred_element_type=jnp.float32
    )
    live_mask = lax.broadcasted_iota(jnp.int32, (group_rows, hist_len), 1) < block_lens[:, None]
    weight = (jnp.where(live_mask[:, :, None], scores, 0.0) * (1.0 / math.sqrt(hist_len))).astype(
        jnp.bfloat16
    )
    head_parts = behavior_emb.reshape(group_rows, hist_len, head_count, feat_width // head_count)
    pooled = jnp.einsum("glh,glhd->ghd", weight, head_parts, preferred_element_type=jnp.float32)
    return pooled.reshape(group_rows, feat_width)


def tower_loss(tower_params, pooled, target, labels, loss_scale):
    w_tower1, b_tower1, w_tower2, b_tower2, w_out = tower_params
    feature = jnp.concatenate([pooled, target.astype(jnp.float32)], axis=-1).astype(jnp.bfloat16)
    hidden_one = jax.nn.silu(
        jnp.dot(feature, w_tower1.astype(jnp.bfloat16), preferred_element_type=jnp.float32)
        + b_tower1
    ).astype(jnp.bfloat16)
    hidden_two = jax.nn.silu(
        jnp.dot(hidden_one, w_tower2.astype(jnp.bfloat16), preferred_element_type=jnp.float32)
        + b_tower2
    ).astype(jnp.bfloat16)
    logits = jnp.dot(hidden_two, w_out.astype(jnp.bfloat16), preferred_element_type=jnp.float32)
    losses = jax.nn.softplus(logits) - labels.astype(jnp.float32) * logits
    return jnp.sum(losses) * loss_scale


def total_loss(behavior_emb, target, unit_params, tower_params, hist_lens, labels, loss_scale):
    user_count, hist_len, feat_width = behavior_emb.shape
    block_count = user_count // BLOCK_USERS
    block_args = (
        behavior_emb.reshape(block_count, BLOCK_USERS, hist_len, feat_width),
        hist_lens.reshape(block_count, BLOCK_USERS),
        target.reshape(block_count, BLOCK_USERS, feat_width),
    )
    one_block = jax.checkpoint(
        lambda parts_in: pool_block(unit_params, parts_in[0], parts_in[1], parts_in[2])
    )
    pooled = lax.map(one_block, block_args).reshape(user_count, feat_width)
    return tower_loss(tower_params, pooled, target, labels, loss_scale)


def owner_ranks(owners, device_count):
    id_count = owners.shape[0]
    block_rows = 512
    block_total = (id_count + block_rows - 1) // block_rows
    padded_owner = jnp.concatenate(
        [owners, jnp.full((block_total * block_rows - id_count,), -1, jnp.int32)]
    )
    owner_numbers = jnp.arange(device_count, dtype=jnp.int32)
    owner_hot = (
        (padded_owner[:, None] == owner_numbers[None, :])
        .astype(jnp.bfloat16)
        .reshape(block_total, block_rows, device_count)
    )
    row_place = lax.broadcasted_iota(jnp.int32, (block_rows, block_rows), 0)
    col_place = lax.broadcasted_iota(jnp.int32, (block_rows, block_rows), 1)
    earlier = (col_place < row_place).astype(jnp.bfloat16)
    within = jnp.einsum("ij,bjd->bid", earlier, owner_hot, preferred_element_type=jnp.float32)
    block_sums = jnp.sum(owner_hot, axis=1, dtype=jnp.float32)
    before = jnp.cumsum(block_sums, axis=0) - block_sums
    rank_float = jnp.einsum(
        "bid,bid->bi", within + before[:, None, :], owner_hot, preferred_element_type=jnp.float32
    )
    return rank_float.reshape(-1)[:id_count].astype(jnp.int32)


def per_device(
    hist_ids,
    hist_lens,
    cand_ids,
    labels,
    item_table,
    w_unit,
    b_unit,
    w_mid,
    b_mid,
    w_head,
    w_tower1,
    b_tower1,
    w_tower2,
    b_tower2,
    w_out,
):
    group_count = lax.axis_size("grp")
    within_count = lax.axis_size("dp")
    device_count = group_count * within_count
    user_count, hist_len = hist_ids.shape
    tab_rows, feat_width = item_table.shape
    loss_scale = 1.0 / math.sqrt(user_count * device_count)
    unit_params = (w_unit, b_unit, w_mid, b_mid, w_head)
    tower_params = (w_tower1, b_tower1, w_tower2, b_tower2, w_out)
    all_ids = jnp.concatenate([hist_ids.reshape(-1), cand_ids])
    id_count = all_ids.shape[0]
    slot_cap = 8 * ((2 * id_count + 8 * device_count - 1) // (8 * device_count))
    owners = all_ids // tab_rows
    bucket_rank = owner_ranks(owners, device_count)
    slot_index = owners * slot_cap + bucket_rank
    owner_numbers = jnp.arange(device_count, dtype=jnp.int32)
    owner_counts = jnp.sum((owners[None, :] == owner_numbers[:, None]).astype(jnp.int32), axis=1)
    slot_numbers = lax.broadcasted_iota(jnp.int32, (device_count, slot_cap), 1)
    filler_keys = jnp.where(
        slot_numbers < slot_cap - owner_counts[:, None],
        (2 * owner_numbers[:, None] + 1) * id_count,
        jnp.iinfo(jnp.int32).max,
    )
    slot_total = device_count * slot_cap
    sort_keys = jnp.concatenate(
        [2 * id_count * owners + jnp.arange(id_count, dtype=jnp.int32), filler_keys.reshape(-1)]
    )
    sort_ids = jnp.concatenate([all_ids, jnp.full((slot_total,), -1, jnp.int32)])
    sorted_keys, sorted_ids = lax.sort((sort_keys, sort_ids), num_keys=1, is_stable=False)
    send_ids = sorted_ids[:slot_total]
    slot_owner = lax.broadcasted_iota(jnp.int32, (device_count, slot_cap), 0).reshape(-1)
    slot_source = jnp.where(
        send_ids >= 0, sorted_keys[:slot_total] - 2 * id_count * slot_owner, id_count
    )
    owned_ids = lax.all_to_all(
        send_ids.reshape(device_count, slot_cap),
        ("grp", "dp"),
        split_axis=0,
        concat_axis=0,
        tiled=True,
    )
    own_index = lax.axis_index(("grp", "dp"))
    local_rows = owned_ids - own_index * tab_rows
    live_slot = owned_ids >= 0
    safe_rows = jnp.clip(local_rows, 0, tab_rows - 1)
    found_rows = item_table[safe_rows].astype(jnp.bfloat16)
    returned = lax.all_to_all(found_rows, ("grp", "dp"), split_axis=0, concat_axis=0, tiled=True)
    all_emb = returned.reshape(device_count * slot_cap, feat_width)[slot_index]
    behavior_emb = all_emb[: user_count * hist_len].reshape(user_count, hist_len, feat_width)
    target = all_emb[user_count * hist_len :]

    def loss_of(emb_in, target_in, unit_in, tower_in):
        return total_loss(emb_in, target_in, unit_in, tower_in, hist_lens, labels, loss_scale)

    local_loss, pullback = jax.vjp(loss_of, behavior_emb, target, unit_params, tower_params)
    d_emb, d_target, unit_grads, tower_grads = pullback(jnp.ones((), jnp.float32))
    all_cot = jnp.concatenate(
        [d_emb.reshape(-1, feat_width), d_target, jnp.zeros((1, feat_width), jnp.bfloat16)], axis=0
    )
    source_by_owner = slot_source.reshape(device_count, slot_cap)
    keyed_rows = jnp.where(live_slot, safe_rows, tab_rows)
    head_cap = 8 * ((slot_cap // 2 + 7) // 8)
    tail_cap = slot_cap - head_cap

    def exchange(first, count):
        sent = all_cot[source_by_owner[:, first : first + count].reshape(-1)]
        return lax.all_to_all(
            sent.reshape(device_count, count, feat_width),
            ("grp", "dp"),
            split_axis=0,
            concat_axis=0,
            tiled=True,
        ).reshape(-1, feat_width)

    def by_row(first, count):
        rows = keyed_rows[:, first : first + count].reshape(-1)
        return lax.sort(
            (rows, jnp.arange(rows.shape[0], dtype=jnp.int32)), num_keys=1, is_stable=False
        )

    def add_rows(table, rows, places, cot):
        cot_sorted = cot[places].astype(jnp.float32) * float(hist_len)
        return table.at[rows].add(cot_sorted, indices_are_sorted=True, mode="drop")

    head_rows, head_places = by_row(0, head_cap)
    tail_rows, tail_places = by_row(head_cap, tail_cap)
    head_cot = exchange(0, head_cap)
    tail_cot = exchange(head_cap, tail_cap)
    table_part = add_rows(
        jnp.zeros((tab_rows, feat_width), jnp.float32), head_rows, head_places, head_cot
    )
    tail_block = device_count * tail_cap // 8
    tail_live = jnp.sum((tail_rows < tab_rows).astype(jnp.int32))

    def tail_step(step, table):
        rows = lax.dynamic_slice_in_dim(tail_rows, step * tail_block, tail_block)
        places = lax.dynamic_slice_in_dim(tail_places, step * tail_block, tail_block)
        return add_rows(table, rows, places, tail_cot)

    table_part = lax.fori_loop(0, (tail_live + tail_block - 1) // tail_block, tail_step, table_part)
    dense_local = (
        unit_grads[0],
        unit_grads[1],
        unit_grads[2],
        unit_grads[3],
        unit_grads[4],
        tower_grads[0],
        tower_grads[1],
        tower_grads[2],
        tower_grads[3],
        tower_grads[4],
        local_loss,
    )
    dense_total = lax.psum(
        (
            dense_local[0],
            dense_local[1],
            dense_local[2],
            dense_local[3],
            dense_local[4],
            dense_local[5],
            dense_local[6],
            dense_local[7],
            dense_local[8],
            dense_local[9],
            dense_local[10],
        ),
        ("grp", "dp"),
    )
    return (
        table_part,
        dense_total[0],
        dense_total[1],
        dense_total[2],
        dense_total[3],
        dense_total[4],
        dense_total[5],
        dense_total[6],
        dense_total[7],
        dense_total[8],
        dense_total[9],
        dense_total[10],
    )


def solution(mesh):
    placed = (
        P(("grp", "dp"), None),
        P(("grp", "dp")),
        P(("grp", "dp")),
        P(("grp", "dp")),
        P(("grp", "dp"), None),
        P(),
        P(),
        P(),
        P(),
        P(),
        P(),
        P(),
        P(),
        P(),
        P(),
    )
    return jax.shard_map(
        per_device,
        mesh=mesh,
        in_specs=placed,
        out_specs=(P(("grp", "dp"), None), P(), P(), P(), P(), P(), P(), P(), P(), P(), P(), P()),
        check_vma=False,
    )
```
